32 devices in a mesh: row: 8 (over z, core), col: 4 (over y, x).
Axes of the slice: x: 2, y: 2, z: 4, core: 2. Of those that a mesh axis runs over, the one named last changes fastest.
Arguments:
- row_desc: bfloat16 [128, 256, 256], P(('row', 'col')), may hold values from -32 to 32, as said below
- col_desc: bfloat16 [32, 256, 256], P(('row', 'col')), may hold values from -32 to 32, as said below
- col_coords: bfloat16 [32, 2, 256], P(('row', 'col')), may hold values from -1 to 1
- row_counts: int32 [128], replicated, may hold values from 64 to 256
- col_counts: int32 [32], replicated, may hold values from 64 to 256
- row_cluster: int32 [128], replicated, may hold values from 0 to 7
- col_cluster: int32 [32], replicated, may hold values from 0 to 7
Outputs:
- matches: float32 [6, 128, 3, 256], P(None, ('row', 'col'))
The draws below stay inside these ranges and needn't reach their ends.
Inputs may be any that keep to these rules, and one draw needn't show every extreme that they name: `row_desc`: custom descriptor draw. `col_desc`: custom descriptor draw.
All inputs are finite; a program needn't handle non-finite values.
Results may differ from the reference program's by a relative error of at most 0.0025.
Values may be sent and summed in bfloat16 or wider, within the bound.
A program may use at most 64 MiB of HBM per device.

```python
import jax
import jax.numpy as jnp
from jax import lax

D = 256
KP = 256
RI = 4
STEPS = 6
CLUSTERS = 8
RIMG = 128
CIMG = 32
N_ROW = 8
N_COL = 4


spread = 0.112


def paired(key):
    key_col = jax.random.fold_in(key, 11)
    key_row = jax.random.fold_in(key, 12)
    column = spread * jax.random.truncated_normal(key_col, -6.0, 6.0, (CIMG, KP, D), jnp.float32)
    rows = spread * jax.random.truncated_normal(key_row, -6.0, 6.0, (RIMG, KP, D), jnp.float32)
    return (rows, column)


def draw_row_desc(key, part):
    return paired(key)[0].astype(jnp.bfloat16)


def draw_col_desc(key, part):
    return paired(key)[1].astype(jnp.bfloat16)


def with_ends(array, stream_key, least, high):
    longest = array.shape.index(max(array.shape))
    spots = []
    for shift in (0, 1):
        where = [jax.random.randint(jax.random.fold_in(stream_key, axis), (), 0, length) for axis, length in enumerate(array.shape)]
        where[longest] = (where[longest] + shift) % array.shape[longest]
        spots.append(tuple(where))
    return array.at[spots[0]].set(least).at[spots[1]].set(high)


def shard_levels(stream_key, dims, pieces, least, top_value):
    loudness, own = 1.0, jax.random.fold_in(stream_key, 6)
    for position, shards_of in pieces:
        draws = jnp.exp(jax.random.uniform(jax.random.fold_in(own, position), (shards_of,), jnp.float32, least / len(pieces), top_value / len(pieces)))
        loudness = loudness * jnp.repeat(draws, dims[position] // shards_of).reshape([-1 if axis == position else 1 for axis in range(len(dims))])
    return loudness


def setup_inputs(seed: int = 0) -> dict:
    streams_of = jax.random.split(jax.random.key(seed), 8)
    row_desc = draw_row_desc(jax.random.fold_in(streams_of[7], 71), 0)
    col_desc = draw_col_desc(jax.random.fold_in(streams_of[7], 71), 0)
    col_coords = jnp.clip(jax.random.uniform(streams_of[2], (CIMG, 2, KP), jnp.float32, -1.0, 1.0) * shard_levels(streams_of[2], (CIMG, 2, KP), ((0, 32),), -0.4, 0.0), -1.0, 1.0).astype(jnp.bfloat16)
    row_counts = with_ends(jax.random.randint(streams_of[3], (RIMG,), max(16, KP // 4), KP + 1), jax.random.fold_in(streams_of[3], 1), max(16, KP // 4), KP).astype(jnp.int32)
    col_counts = with_ends(jax.random.randint(streams_of[4], (CIMG,), max(16, KP // 4), KP + 1), jax.random.fold_in(streams_of[4], 1), max(16, KP // 4), KP).astype(jnp.int32)
    row_cluster = with_ends(jax.random.randint(streams_of[5], (RIMG,), 0, CLUSTERS), jax.random.fold_in(streams_of[5], 1), 0, CLUSTERS - 1).astype(jnp.int32)
    col_cluster = with_ends(jax.random.randint(streams_of[6], (CIMG,), 0, CLUSTERS), jax.random.fold_in(streams_of[6], 1), 0, CLUSTERS - 1).astype(jnp.int32)
    return {"row_desc": row_desc, "col_desc": col_desc, "col_coords": col_coords, "row_counts": row_counts, "col_counts": col_counts, "row_cluster": row_cluster, "col_cluster": col_cluster}


inv_temp = 10.0
big_value = 1.0e30


def match_pair(rows, column, table, row_count, col_count):
    scores = inv_temp * jnp.dot(rows, column.T, preferred_element_type=jnp.float32)
    places = jnp.arange(rows.shape[0], dtype=jnp.int32)
    row_valid = (places < row_count)[:, None]
    col_valid = (places < col_count)[None, :]
    row_top = jnp.max(jnp.where(col_valid, scores, -big_value), axis=1, keepdims=True)
    col_top = jnp.max(jnp.where(row_valid, scores, -big_value), axis=0, keepdims=True)
    row_exp = jnp.where(col_valid, jnp.exp(jnp.where(col_valid, scores - row_top, 0.0)), 0.0)
    col_exp = jnp.where(row_valid, jnp.exp(jnp.where(row_valid, scores - col_top, 0.0)), 0.0)
    prob = (row_exp / jnp.sum(row_exp, axis=1, keepdims=True)) * (col_exp / jnp.sum(col_exp, axis=0, keepdims=True))
    prob = prob.astype(jnp.bfloat16)
    return lax.dot_general(table, prob, (((1,), (1,)), ((), ())), preferred_element_type=jnp.float32)


def reference(row_desc, col_desc, col_coords, row_counts, col_counts, row_cluster, col_cluster):
    ones = jnp.ones((col_coords.shape[0], 1, KP), jnp.bfloat16)
    tables = jnp.concatenate([ones, col_coords], axis=1)
    results = []
    for step in range(STEPS):
        def single(flat):
            block = flat // RI
            within = flat % RI
            row_pos = block // N_COL
            col_pos = block % N_COL
            image = ((row_pos * N_COL + (col_pos - step) % N_COL) * RI + within).astype(jnp.int32)
            other = (((row_pos - step) % N_ROW) * N_COL + col_pos).astype(jnp.int32)

            def working(unused):
                return match_pair(row_desc[image], col_desc[other], tables[other], row_counts[image], col_counts[other])

            def skipped(unused):
                return jnp.zeros((3, KP), jnp.float32)

            return lax.cond(row_cluster[image] == col_cluster[other], working, skipped, 0)

        results.append(lax.map(single, jnp.arange(N_ROW * N_COL * RI, dtype=jnp.int32)))
    return jnp.stack(results)
```

```python
import functools

import jax
import jax.numpy as jnp
from jax import lax
from jax.experimental import pallas as pl
from jax.experimental.pallas import tpu as pltpu
from jax.sharding import PartitionSpec as P

STEPS = 6
HOP = 2
PIECES = 2

scale = 10.0 * 1.4426950408889634
big_value = 1e30
MESH = pl.DeviceIdType.MESH


def match_pair(rows, column, table, q_valid, k_valid, q_shown, factor):
    scores = scale * lax.dot_general(
        rows, column, (((1,), (1,)), ((), ())), preferred_element_type=jnp.float32
    )
    scores = jnp.where(jnp.logical_and(q_valid, k_valid), scores, -big_value)
    row_top = jnp.max(scores, axis=1, keepdims=True)
    col_top = jnp.max(scores, axis=0, keepdims=True)
    row_exp = jnp.exp2(scores - row_top)
    col_exp = jnp.exp2(scores - col_top)
    row_inv = 1.0 / jnp.sum(row_exp, axis=1, keepdims=True)
    col_inv = 1.0 / jnp.sum(col_exp, axis=0, keepdims=True)
    prob = ((row_exp * row_inv) * (col_exp * col_inv)).astype(jnp.bfloat16)
    result = lax.dot_general(
        table, prob, (((1,), (1,)), ((), ())), preferred_element_type=jnp.float32
    )
    return jnp.where(q_shown, result, 0.0) * factor


def kernel(
    n_row,
    n_col,
    row_counts,
    col_counts,
    row_cluster,
    col_cluster,
    rows_hbm,
    col_hbm,
    coords_hbm,
    out_ref,
    rows_ref,
    col_ref,
    coords_ref,
    load_sem,
    relay,
    relay_coords,
    image,
    coords,
    result,
    relay_send,
    relay_recv,
    image_send,
    image_recv,
    result_send,
    result_recv,
):
    loads = [
        pltpu.make_async_copy(src, dst, load_sem.at[at])
        for at, (src, dst) in enumerate(
            ((rows_hbm, rows_ref), (col_hbm, col_ref), (coords_hbm, coords_ref))
        )
    ]
    row = lax.axis_index("row")
    col = lax.axis_index("col")
    core = lax.rem(row, HOP)
    panel = rows_ref.shape[0]
    slots = rows_ref.shape[1]
    piece = slots // PIECES

    def place(drow, dcol):
        return (lax.rem(row + drow + n_row, n_row), lax.rem(col + dcol % n_col, n_col))

    def hops_of(step, parity):
        return (step + parity) // HOP

    def shared(step, parity):
        hop = hops_of(step, parity)
        return sum(hops_of(other, parity) == hop for other in range(1, STEPS)) > 1

    hops = [
        max(hops_of(step, parity) for step in range(1, STEPS) if shared(step, parity))
        for parity in range(HOP)
    ]

    def straight(step, parity):
        return hops_of(step, parity) > hops[parity]


    def lateral(step, parity):
        if straight(step, parity):
            return (step, -step)
        return (step - hops_of(step, parity) * HOP, -step)

    def stays(step):
        return step % HOP == 0 and step % n_col == 0

    across = sorted({(-step) % n_col for step in range(1, STEPS) if step % HOP})
    along = {(-step) % n_col for step in range(1, STEPS) if step % HOP == 0}
    along |= {step % n_col for step in range(1, STEPS)}
    along = sorted(along - {0})
    other = 1 - 2 * core
    barrier = pltpu.get_barrier_semaphore()
    sources = [place((-HOP * (hop + 1)) % n_row, 0) for hop in range(max(hops))]
    sources += [place(other, -dcol) for dcol in across]
    sources += [place(0, -dcol) for dcol in along]
    far = sorted({step for step in range(1, STEPS) for parity in range(HOP) if straight(step, parity)})
    sources += [place((-step) % n_row, step) for step in far]
    for source in sources:
        pl.semaphore_signal(barrier, inc=1, device_id=source, device_id_type=MESH)
    for load in loads:
        load.start()
    pl.semaphore_wait(barrier, len(sources))

    def view(ref, part):
        return ref.at[pl.ds(part * piece, piece)]

    def remote(src, dst, send, recv, drow, dcol):
        return pltpu.make_async_remote_copy(
            src_ref=src,
            dst_ref=dst,
            send_sem=send,
            recv_sem=recv,
            device_id=place(drow, dcol),
            device_id_type=MESH,
        )

    def source_of(hop, part):
        if part == PIECES:
            return coords_hbm.at[0] if hop == 0 else relay_coords.at[hop - 1]
        return view(col_hbm.at[0] if hop == 0 else relay.at[hop - 1], part)

    def relay_copy(hop, part):
        dst = relay_coords.at[hop] if part == PIECES else view(relay.at[hop], part)
        return remote(
            source_of(0, part),
            dst,
            relay_send.at[hop, part],
            relay_recv.at[hop, part],
            HOP * (hop + 1),
            0,
        )

    def image_copy(step, parity, part):
        slot = step - 1
        dst = coords.at[slot] if part == PIECES else view(image.at[slot], part)
        return remote(
            source_of(0 if straight(step, parity) else hops_of(step, parity), part),
            dst,
            image_send.at[slot, part],
            image_recv.at[slot, part],
            *lateral(step, parity),
        )

    def back_copy(step):
        return remote(
            result.at[step], out_ref.at[step], result_send.at[step], result_recv.at[step], 0, step
        )

    parts = [PIECES] + list(range(PIECES))

    def on_cores(which, body):
        for parity in which:
            pl.when(core == parity)(functools.partial(body, parity))

    def relay_cores(hop):
        return [parity for parity in range(HOP) if hop < hops[parity]]

    def for_relay(hop, body):
        if len(relay_cores(hop)) == HOP:
            body()
        elif relay_cores(hop):
            on_cores(relay_cores(hop), lambda parity: body())

    def pass_on(hop, part):
        def hand(parity):
            for step in range(1, STEPS):
                if hops_of(step, parity) == hop and not straight(step, parity) and not stays(step):
                    image_copy(step, parity, part).start()

        on_cores(range(HOP), hand)

    def take(hop):
        for part in parts:

            def one():
                relay_copy(hop, part).wait_recv()
                pass_on(hop + 1, part)

            for_relay(hop, one)

    for part in parts:
        pass_on(0, part)
        for_relay(0, lambda: relay_copy(0, part).start())
    for hop in range(1, max(hops)):
        for part in parts:
            for_relay(hop, lambda: relay_copy(hop, part).start())

    def send_straight(parity):
        for step in range(1, STEPS):
            for part in parts:
                if straight(step, parity):
                    image_copy(step, parity, part).start()

    on_cores(range(HOP), send_straight)
    for load in loads:
        load.wait()
    own_block = row * n_col + col
    tall_place = lax.broadcasted_iota(jnp.int32, (slots, 1), 0)
    wide_place = lax.broadcasted_iota(jnp.int32, (1, slots), 1)

    def settle(step):
        if step and not stays(step):
            for part in parts:
                image_copy(step, 0, part).wait_recv()

    def match(step, within_range):
        if step == 0:
            column_ref, points_ref = col_ref.at[0], coords_ref.at[0]
        elif stays(step):
            hop = hops_of(step, 0) - 1
            column_ref, points_ref = relay.at[hop], relay_coords.at[hop]
        else:
            column_ref, points_ref = image.at[step - 1], coords.at[step - 1]
        col_image = lax.rem(row + (-step) % n_row, n_row) * n_col + lax.rem(col + step % n_col, n_col)
        col_count = col_counts[col_image]
        col_group = col_cluster[col_image]
        k_valid = wide_place < col_count
        points_now = points_ref[...].astype(jnp.float32)
        table = jnp.concatenate([jnp.ones((1, slots), jnp.float32), points_now], axis=0)
        table = jnp.where(k_valid, table, 0.0).astype(jnp.bfloat16)
        dst = out_ref if step % n_col == 0 else result
        for within in within_range:
            index = own_block * panel + within
            factor = jnp.where(row_cluster[index] == col_group, 1.0, 0.0)
            dst[step, :, within] = match_pair(
                rows_ref[within],
                column_ref[...],
                table,
                tall_place < row_counts[index],
                k_valid,
                wide_place < row_counts[index],
                factor,
            )

    half = panel // 2
    first, second = range(half), range(half, panel)
    remote_steps = [step for step in range(1, STEPS) if step % n_col]
    order = [0] + remote_steps[:2] + remote_steps[:1:-1] + [step for step in range(1, STEPS) if step % n_col == 0]
    pending = None
    match(0, first)
    for at, step in enumerate(order):
        settle(step)
        if at:
            match(step, first)
        if pending is not None:
            back_copy(pending).start()
            pending = None
        if step % n_col:
            pending = step
        if at == 0:
            match(step, second)
            take(at)
        elif at < max(hops):
            take(at)
            match(step, second)
        else:
            match(step, second)
    if pending is not None:
        back_copy(pending).start()

    for part in parts:
        for hop in range(max(hops)):
            for_relay(hop, lambda: relay_copy(hop, part).wait_send())
        for step in range(1, STEPS):
            if not stays(step):
                image_copy(step, 0, part).wait_send()
    for step in range(1, STEPS):
        if step % n_col:
            back_copy(step).wait()


def local(row_desc, col_desc, col_coords, row_counts, col_counts, row_cluster, col_cluster):
    n_row = lax.axis_size("row")
    n_col = lax.axis_size("col")
    panel, slots, width = row_desc.shape
    smem = pl.BlockSpec(memory_space=pltpu.SMEM)
    vmem = pl.BlockSpec(memory_space=pltpu.VMEM)
    dma = pltpu.SemaphoreType.DMA
    result = pl.pallas_call(
        functools.partial(kernel, n_row, n_col),
        out_shape=pltpu.VMEM((STEPS, 3, panel, slots), jnp.float32),
        in_specs=[smem] * 4 + [pl.BlockSpec(memory_space=pl.ANY)] * 3,
        out_specs=vmem,
        scratch_shapes=[
            pltpu.VMEM(row_desc.shape, row_desc.dtype),
            pltpu.VMEM(col_desc.shape, col_desc.dtype),
            pltpu.VMEM(col_coords.shape, col_coords.dtype),
            dma((3,)),
            pltpu.VMEM((STEPS // HOP, slots, width), jnp.bfloat16),
            pltpu.VMEM((STEPS // HOP, 2, slots), jnp.bfloat16),
            pltpu.VMEM((STEPS - 1, slots, width), jnp.bfloat16),
            pltpu.VMEM((STEPS - 1, 2, slots), jnp.bfloat16),
            pltpu.VMEM((STEPS, 3, panel, slots), jnp.float32),
            dma((STEPS // HOP, PIECES + 1)),
            dma((STEPS // HOP, PIECES + 1)),
            dma((STEPS - 1, PIECES + 1)),
            dma((STEPS - 1, PIECES + 1)),
            dma((STEPS,)),
            dma((STEPS,)),
        ],
        compiler_params=pltpu.CompilerParams(collective_id=0, has_side_effects=True),
        name="match",
    )(row_counts, col_counts, row_cluster, col_cluster, row_desc, col_desc, col_coords)
    return jnp.transpose(result, (0, 2, 1, 3))


def solution(mesh):
    return jax.shard_map(
        local,
        mesh=mesh,
        in_specs=(
            P(("row", "col"), None, None),
            P(("row", "col"), None, None),
            P(("row", "col"), None, None),
            P(),
            P(),
            P(),
            P(),
        ),
        out_specs=P(None, ("row", "col"), None, None),
        check_vma=False,
    )
```

```python
import functools

import jax
import jax.numpy as jnp
from jax import lax
from jax.experimental import pallas as pl
from jax.experimental.pallas import tpu as pltpu
from jax.sharding import PartitionSpec as P

STEPS = 6
HOP = 2
PIECES = 2
ORDERS = ((1, 2, 5, 3), (1, 2, 3, 5))

scale = 10.0 * 1.4426950408889634
big_value = 1e30
MESH = pl.DeviceIdType.MESH


def match_pair(rows, column, table, q_valid, k_valid, q_shown, factor):
    scores = scale * lax.dot_general(
        rows, column, (((1,), (1,)), ((), ())), preferred_element_type=jnp.float32
    )
    scores = jnp.where(jnp.logical_and(q_valid, k_valid), scores, -big_value)
    row_top = jnp.max(scores, axis=1, keepdims=True)
    col_top = jnp.max(scores, axis=0, keepdims=True)
    row_exp = jnp.exp2(scores - row_top)
    col_exp = jnp.exp2(scores - col_top)
    row_inv = 1.0 / jnp.sum(row_exp, axis=1, keepdims=True)
    col_inv = 1.0 / jnp.sum(col_exp, axis=0, keepdims=True)
    prob = ((row_exp * row_inv) * (col_exp * col_inv)).astype(jnp.bfloat16)
    result = lax.dot_general(
        table, prob, (((1,), (1,)), ((), ())), preferred_element_type=jnp.float32
    )
    return jnp.where(q_shown, result, 0.0) * factor


def kernel(
    n_row,
    n_col,
    row_counts_hbm,
    col_counts_hbm,
    row_cluster_hbm,
    col_cluster_hbm,
    rows_hbm,
    col_hbm,
    coords_hbm,
    out_ref,
    rows_ref,
    col_ref,
    coords_ref,
    row_counts,
    col_counts,
    row_cluster,
    col_cluster,
    load_sem,
    relay,
    relay_coords,
    image,
    coords,
    result,
    relay_send,
    relay_recv,
    image_send,
    image_recv,
    result_send,
    result_recv,
):
    loads = [
        pltpu.make_async_copy(src, dst, load_sem.at[at])
        for at, (src, dst) in enumerate(
            (
                (rows_hbm, rows_ref),
                (col_hbm, col_ref),
                (coords_hbm, coords_ref),
                (row_counts_hbm, row_counts),
                (col_counts_hbm, col_counts),
                (row_cluster_hbm, row_cluster),
                (col_cluster_hbm, col_cluster),
            )
        )
    ]
    row = lax.axis_index("row")
    col = lax.axis_index("col")
    core = lax.rem(row, HOP)
    panel = rows_ref.shape[0]
    slots = rows_ref.shape[1]
    piece = slots // PIECES

    def place(drow, dcol):
        dcol = dcol % n_col if isinstance(dcol, int) else dcol
        return (lax.rem(row + drow + n_row, n_row), lax.rem(col + dcol, n_col))

    def hops_of(step, parity):
        return (step + parity) // HOP

    def shared(step, parity):
        hop = hops_of(step, parity)
        return sum(hops_of(other, parity) == hop for other in range(1, STEPS)) > 1

    hops = [
        max(hops_of(step, parity) for step in range(1, STEPS) if shared(step, parity))
        for parity in range(HOP)
    ]

    def straight(step, parity):
        return hops_of(step, parity) > hops[parity]


    def lateral(step, parity):
        if straight(step, parity):
            return (step, -step)
        return (step - hops_of(step, parity) * HOP, -step)

    def stays(step):
        return step % HOP == 0 and step % n_col == 0

    across = sorted({(-step) % n_col for step in range(1, STEPS) if step % HOP})
    along = {(-step) % n_col for step in range(1, STEPS) if step % HOP == 0}
    along |= {step % n_col for step in range(1, STEPS)}
    along = sorted(along - {0})
    other = 1 - 2 * core
    barrier = pltpu.get_barrier_semaphore()
    sources = [place((-HOP * (hop + 1)) % n_row, 0) for hop in range(max(hops))]
    sources += [place(other, -dcol) for dcol in across]
    sources += [place(0, -dcol) for dcol in along]
    far = sorted({step for step in range(1, STEPS) for parity in range(HOP) if straight(step, parity)})
    sources += [place((-step) % n_row, step) for step in far]
    for source in sources:
        pl.semaphore_signal(barrier, inc=1, device_id=source, device_id_type=MESH)
    for load in loads:
        load.start()
    pl.semaphore_wait(barrier, len(sources))

    def view(ref, part):
        return ref.at[pl.ds(part * piece, piece)]

    def remote(src, dst, send, recv, drow, dcol):
        return pltpu.make_async_remote_copy(
            src_ref=src,
            dst_ref=dst,
            send_sem=send,
            recv_sem=recv,
            device_id=place(drow, dcol),
            device_id_type=MESH,
        )

    def source_of(hop, part):
        if part == PIECES:
            return coords_hbm.at[0] if hop == 0 else relay_coords.at[hop - 1]
        return view(col_hbm.at[0] if hop == 0 else relay.at[hop - 1], part)

    def relay_copy(hop, part):
        dst = relay_coords.at[hop] if part == PIECES else view(relay.at[hop], part)
        return remote(
            source_of(0, part),
            dst,
            relay_send.at[hop, part],
            relay_recv.at[hop, part],
            HOP * (hop + 1),
            0,
        )

    def image_copy(step, parity, part):
        slot = step - 1
        dst = coords.at[slot] if part == PIECES else view(image.at[slot], part)
        return remote(
            source_of(0 if straight(step, parity) else hops_of(step, parity), part),
            dst,
            image_send.at[slot, part],
            image_recv.at[slot, part],
            *lateral(step, parity),
        )

    def back_copy(step):
        return remote(
            result.at[step], out_ref.at[step], result_send.at[step], result_recv.at[step], 0, step
        )

    parts = [PIECES] + list(range(PIECES))

    def on_cores(which, body):
        for parity in which:
            pl.when(core == parity)(functools.partial(body, parity))

    def relay_cores(hop):
        return [parity for parity in range(HOP) if hop < hops[parity]]

    def for_relay(hop, body):
        if len(relay_cores(hop)) == HOP:
            body()
        elif relay_cores(hop):
            on_cores(relay_cores(hop), lambda parity: body())

    def pass_on(hop, part):
        def hand(parity):
            for step in range(1, STEPS):
                if hops_of(step, parity) == hop and not straight(step, parity) and not stays(step):
                    image_copy(step, parity, part).start()

        on_cores(range(HOP), hand)

    def take(hop):
        for part in parts:

            def one():
                relay_copy(hop, part).wait_recv()
                pass_on(hop + 1, part)

            for_relay(hop, one)

    for part in parts:
        pass_on(0, part)
        for_relay(0, lambda: relay_copy(0, part).start())
    for hop in range(1, max(hops)):
        for part in parts:
            for_relay(hop, lambda: relay_copy(hop, part).start())

    def send_straight(parity):
        for step in range(1, STEPS):
            for part in parts:
                if straight(step, parity):
                    image_copy(step, parity, part).start()

    on_cores(range(HOP), send_straight)
    for load in loads:
        load.wait()
    own_block = row * n_col + col
    tall_place = lax.broadcasted_iota(jnp.int32, (slots, 1), 0)
    wide_place = lax.broadcasted_iota(jnp.int32, (1, slots), 1)

    def settle(step):
        if not isinstance(step, int):
            for part in parts:
                slot = step - 1
                dst = coords.at[slot] if part == PIECES else view(image.at[slot], part)
                remote(
                    dst, dst, image_send.at[slot, part], image_recv.at[slot, part], 0, 1
                ).wait_recv()

    def match(step, within_range):
        if isinstance(step, int) and step == 0:
            column_ref, points_ref = col_ref.at[0], coords_ref.at[0]
        elif isinstance(step, int):
            hop = hops_of(step, 0) - 1
            column_ref, points_ref = relay.at[hop], relay_coords.at[hop]
        else:
            column_ref, points_ref = image.at[step - 1], coords.at[step - 1]
        col_image = lax.rem(row + n_row - step, n_row) * n_col + lax.rem(col + step, n_col)
        col_count = col_counts[col_image]
        col_group = col_cluster[col_image]
        k_valid = wide_place < col_count
        points_now = points_ref[...].astype(jnp.float32)
        table = jnp.concatenate([jnp.ones((1, slots), jnp.float32), points_now], axis=0)
        table = jnp.where(k_valid, table, 0.0).astype(jnp.bfloat16)
        dst = out_ref if isinstance(step, int) else result
        for within in within_range:
            index = own_block * panel + within
            factor = jnp.where(row_cluster[index] == col_group, 1.0, 0.0)
            dst[step, :, within] = match_pair(
                rows_ref[within],
                column_ref[...],
                table,
                tall_place < row_counts[index],
                k_valid,
                wide_place < row_counts[index],
                factor,
            )

    remote_steps = [step for step in range(1, STEPS) if step % n_col]
    orders = [[*order, *(step for step in remote_steps if step not in order)] for order in ORDERS]
    order = [0]
    order += [jnp.where(core == 0, left, right) for left, right in zip(*orders)]
    order += [step for step in range(1, STEPS) if step % n_col == 0]
    whole = range(panel)
    match(0, whole)
    for hop in range(max(hops)):
        take(hop)
    for step in order[1:]:
        settle(step)
        match(step, whole)
        if not isinstance(step, int):
            back_copy(step).start()

    for part in parts:
        for hop in range(max(hops)):
            for_relay(hop, lambda: relay_copy(hop, part).wait_send())
        for step in range(1, STEPS):
            if not stays(step):
                image_copy(step, 0, part).wait_send()
    for step in range(1, STEPS):
        if step % n_col:
            back_copy(step).wait()


def local(row_desc, col_desc, col_coords, row_counts, col_counts, row_cluster, col_cluster):
    n_row = lax.axis_size("row")
    n_col = lax.axis_size("col")
    panel, slots, width = row_desc.shape
    vmem = pl.BlockSpec(memory_space=pltpu.VMEM)
    dma = pltpu.SemaphoreType.DMA
    result = pl.pallas_call(
        functools.partial(kernel, n_row, n_col),
        out_shape=pltpu.VMEM((STEPS, 3, panel, slots), jnp.float32),
        in_specs=[pl.BlockSpec(memory_space=pl.ANY)] * 7,
        out_specs=vmem,
        scratch_shapes=[
            pltpu.VMEM(row_desc.shape, row_desc.dtype),
            pltpu.VMEM(col_desc.shape, col_desc.dtype),
            pltpu.VMEM(col_coords.shape, col_coords.dtype),
            pltpu.SMEM(row_counts.shape, row_counts.dtype),
            pltpu.SMEM(col_counts.shape, col_counts.dtype),
            pltpu.SMEM(row_cluster.shape, row_cluster.dtype),
            pltpu.SMEM(col_cluster.shape, col_cluster.dtype),
            dma((7,)),
            pltpu.VMEM((STEPS // HOP, slots, width), jnp.bfloat16),
            pltpu.VMEM((STEPS // HOP, 2, slots), jnp.bfloat16),
            pltpu.VMEM((STEPS - 1, slots, width), jnp.bfloat16),
            pltpu.VMEM((STEPS - 1, 2, slots), jnp.bfloat16),
            pltpu.VMEM((STEPS, 3, panel, slots), jnp.float32),
            dma((STEPS // HOP, PIECES + 1)),
            dma((STEPS // HOP, PIECES + 1)),
            dma((STEPS - 1, PIECES + 1)),
            dma((STEPS - 1, PIECES + 1)),
            dma((STEPS,)),
            dma((STEPS,)),
        ],
        compiler_params=pltpu.CompilerParams(collective_id=0, has_side_effects=True),
        name="match",
    )(row_counts, col_counts, row_cluster, col_cluster, row_desc, col_desc, col_coords)
    return jnp.transpose(result, (0, 2, 1, 3))


def solution(mesh):
    return jax.shard_map(
        local,
        mesh=mesh,
        in_specs=(
            P(("row", "col"), None, None),
            P(("row", "col"), None, None),
            P(("row", "col"), None, None),
            P(),
            P(),
            P(),
            P(),
        ),
        out_specs=P(None, ("row", "col"), None, None),
        check_vma=False,
    )
```

```python
import functools

import jax
import jax.numpy as jnp
from jax import lax
from jax.experimental import pallas as pl
from jax.experimental.pallas import tpu as pltpu
from jax.sharding import PartitionSpec as P

STEPS = 6
HOP = 2
PIECES = 4
ORDERS = ((1, 2, 5, 3), (1, 2, 3, 5))

scale = 10.0 * 1.4426950408889634
big_value = 1e30
MESH = pl.DeviceIdType.MESH


def match_pair(rows, column, table, q_valid, k_valid, q_shown, factor):
    scores = scale * lax.dot_general(
        rows, column, (((1,), (1,)), ((), ())), preferred_element_type=jnp.float32
    )
    scores = jnp.where(jnp.logical_and(q_valid, k_valid), scores, -big_value)
    row_top = jnp.max(scores, axis=1, keepdims=True)
    col_top = jnp.max(scores, axis=0, keepdims=True)
    row_exp = jnp.exp2(scores - row_top)
    col_exp = jnp.exp2(scores - col_top)
    row_inv = 1.0 / jnp.sum(row_exp, axis=1, keepdims=True)
    col_inv = 1.0 / jnp.sum(col_exp, axis=0, keepdims=True)
    prob = ((row_exp * row_inv) * (col_exp * col_inv)).astype(jnp.bfloat16)
    result = lax.dot_general(
        table, prob, (((1,), (1,)), ((), ())), preferred_element_type=jnp.float32
    )
    return jnp.where(q_shown, result, 0.0) * factor


def kernel(
    n_row,
    n_col,
    row_counts_hbm,
    col_counts_hbm,
    row_cluster_hbm,
    col_cluster_hbm,
    rows_hbm,
    col_hbm,
    coords_hbm,
    out_ref,
    rows_ref,
    col_ref,
    coords_ref,
    row_counts,
    col_counts,
    row_cluster,
    col_cluster,
    load_sem,
    relay,
    relay_coords,
    image,
    coords,
    result,
    relay_send,
    relay_recv,
    image_send,
    image_recv,
    result_send,
    result_recv,
):
    loads = [
        pltpu.make_async_copy(src, dst, load_sem.at[at])
        for at, (src, dst) in enumerate(
            (
                (rows_hbm, rows_ref),
                (col_hbm, col_ref),
                (coords_hbm, coords_ref),
                (row_counts_hbm, row_counts),
                (col_counts_hbm, col_counts),
                (row_cluster_hbm, row_cluster),
                (col_cluster_hbm, col_cluster),
            )
        )
    ]
    row = lax.axis_index("row")
    col = lax.axis_index("col")
    core = lax.rem(row, HOP)
    panel = rows_ref.shape[0]
    slots = rows_ref.shape[1]
    piece = slots // PIECES

    def place(drow, dcol):
        dcol = dcol % n_col if isinstance(dcol, int) else dcol
        return (lax.rem(row + drow + n_row, n_row), lax.rem(col + dcol, n_col))

    def hops_of(step, parity):
        return (step + parity) // HOP

    def shared(step, parity):
        hop = hops_of(step, parity)
        return sum(hops_of(other, parity) == hop for other in range(1, STEPS)) > 1

    hops = [
        max(hops_of(step, parity) for step in range(1, STEPS) if shared(step, parity))
        for parity in range(HOP)
    ]

    def straight(step, parity):
        return hops_of(step, parity) > hops[parity]


    def lateral(step, parity):
        if straight(step, parity):
            return (step, -step)
        return (step - hops_of(step, parity) * HOP, -step)

    def stays(step):
        return step % HOP == 0 and step % n_col == 0

    across = sorted({(-step) % n_col for step in range(1, STEPS) if step % HOP})
    along = {(-step) % n_col for step in range(1, STEPS) if step % HOP == 0}
    along |= {step % n_col for step in range(1, STEPS)}
    along = sorted(along - {0})
    other = 1 - 2 * core
    barrier = pltpu.get_barrier_semaphore()
    sources = [place((-HOP * (hop + 1)) % n_row, 0) for hop in range(max(hops))]
    sources += [place(other, -dcol) for dcol in across]
    sources += [place(0, -dcol) for dcol in along]
    far = sorted({step for step in range(1, STEPS) for parity in range(HOP) if straight(step, parity)})
    sources += [place((-step) % n_row, step) for step in far]
    for source in sources:
        pl.semaphore_signal(barrier, inc=1, device_id=source, device_id_type=MESH)
    for load in loads:
        load.start()
    pl.semaphore_wait(barrier, len(sources))

    def view(ref, part):
        return ref.at[pl.ds(part * piece, piece)]

    def remote(src, dst, send, recv, drow, dcol):
        return pltpu.make_async_remote_copy(
            src_ref=src,
            dst_ref=dst,
            send_sem=send,
            recv_sem=recv,
            device_id=place(drow, dcol),
            device_id_type=MESH,
        )

    def source_of(hop, part):
        if part == PIECES:
            return coords_hbm.at[0] if hop == 0 else relay_coords.at[hop - 1]
        return view(col_hbm.at[0] if hop == 0 else relay.at[hop - 1], part)

    def relay_copy(hop, part):
        dst = relay_coords.at[hop] if part == PIECES else view(relay.at[hop], part)
        return remote(
            source_of(0, part),
            dst,
            relay_send.at[hop, part],
            relay_recv.at[hop, part],
            HOP * (hop + 1),
            0,
        )

    def image_copy(step, parity, part):
        slot = step - 1
        dst = coords.at[slot] if part == PIECES else view(image.at[slot], part)
        return remote(
            source_of(0 if straight(step, parity) else hops_of(step, parity), part),
            dst,
            image_send.at[slot, part],
            image_recv.at[slot, part],
            *lateral(step, parity),
        )

    def back_copy(step):
        return remote(
            result.at[step], out_ref.at[step], result_send.at[step], result_recv.at[step], 0, step
        )

    parts = [PIECES] + list(range(PIECES))

    def on_cores(which, body):
        for parity in which:
            pl.when(core == parity)(functools.partial(body, parity))

    def relay_cores(hop):
        return [parity for parity in range(HOP) if hop < hops[parity]]

    def for_relay(hop, body):
        if len(relay_cores(hop)) == HOP:
            body()
        elif relay_cores(hop):
            on_cores(relay_cores(hop), lambda parity: body())

    def pass_on(hop, part):
        def hand(parity):
            for step in range(1, STEPS):
                if hops_of(step, parity) == hop and not straight(step, parity) and not stays(step):
                    image_copy(step, parity, part).start()

        on_cores(range(HOP), hand)

    def take(hop):
        for part in parts:

            def one():
                relay_copy(hop, part).wait_recv()
                pass_on(hop + 1, part)

            for_relay(hop, one)

    for part in parts:
        for_relay(0, lambda: relay_copy(0, part).start())
    for part in parts:
        pass_on(0, part)
    for hop in range(1, max(hops)):
        for part in parts:
            for_relay(hop, lambda: relay_copy(hop, part).start())

    def send_straight(parity):
        for step in range(1, STEPS):
            for part in parts:
                if straight(step, parity):
                    image_copy(step, parity, part).start()

    for load in loads:
        load.wait()
    own_block = row * n_col + col
    tall_place = lax.broadcasted_iota(jnp.int32, (slots, 1), 0)
    wide_place = lax.broadcasted_iota(jnp.int32, (1, slots), 1)

    def settle(step):
        if not isinstance(step, int):
            for part in parts:
                slot = step - 1
                dst = coords.at[slot] if part == PIECES else view(image.at[slot], part)
                remote(
                    dst, dst, image_send.at[slot, part], image_recv.at[slot, part], 0, 1
                ).wait_recv()

    def match(step, within_range):
        if isinstance(step, int) and step == 0:
            column_ref, points_ref = col_ref.at[0], coords_ref.at[0]
        elif isinstance(step, int):
            hop = hops_of(step, 0) - 1
            column_ref, points_ref = relay.at[hop], relay_coords.at[hop]
        else:
            column_ref, points_ref = image.at[step - 1], coords.at[step - 1]
        col_image = lax.rem(row + n_row - step, n_row) * n_col + lax.rem(col + step, n_col)
        col_count = col_counts[col_image]
        col_group = col_cluster[col_image]
        k_valid = wide_place < col_count
        points_now = points_ref[...].astype(jnp.float32)
        table = jnp.concatenate([jnp.ones((1, slots), jnp.float32), points_now], axis=0)
        table = jnp.where(k_valid, table, 0.0).astype(jnp.bfloat16)
        dst = out_ref if isinstance(step, int) else result
        for within in within_range:
            index = own_block * panel + within
            factor = jnp.where(row_cluster[index] == col_group, 1.0, 0.0)
            dst[step, :, within] = match_pair(
                rows_ref[within],
                column_ref[...],
                table,
                tall_place < row_counts[index],
                k_valid,
                wide_place < row_counts[index],
                factor,
            )

    remote_steps = [step for step in range(1, STEPS) if step % n_col]
    orders = [[*order, *(step for step in remote_steps if step not in order)] for order in ORDERS]
    order = [0]
    order += [jnp.where(core == 0, left, right) for left, right in zip(*orders)]
    order += [step for step in range(1, STEPS) if step % n_col == 0]
    whole = range(panel)
    match(0, whole)
    on_cores(range(HOP), send_straight)
    plan = ((0, 1), (0, 1))

    def serve(at):
        def turn(parity):
            for hop in range(max(hops)):
                if hop < len(plan[parity]):
                    if plan[parity][hop] == at:
                        take(hop)
                elif at == 1:
                    take(hop)

        on_cores(range(HOP), turn)

    for at, step in enumerate(order[1:]):
        serve(at)
        settle(step)
        match(step, whole)
        if not isinstance(step, int):
            back_copy(step).start()

    for part in parts:
        for hop in range(max(hops)):
            for_relay(hop, lambda: relay_copy(hop, part).wait_send())
        for step in range(1, STEPS):
            if not stays(step):
                image_copy(step, 0, part).wait_send()
    for step in range(1, STEPS):
        if step % n_col:
            back_copy(step).wait()


def local(row_desc, col_desc, col_coords, row_counts, col_counts, row_cluster, col_cluster):
    n_row = lax.axis_size("row")
    n_col = lax.axis_size("col")
    panel, slots, width = row_desc.shape
    vmem = pl.BlockSpec(memory_space=pltpu.VMEM)
    dma = pltpu.SemaphoreType.DMA
    result = pl.pallas_call(
        functools.partial(kernel, n_row, n_col),
        out_shape=pltpu.VMEM((STEPS, 3, panel, slots), jnp.float32),
        in_specs=[pl.BlockSpec(memory_space=pl.ANY)] * 7,
        out_specs=vmem,
        scratch_shapes=[
            pltpu.VMEM(row_desc.shape, row_desc.dtype),
            pltpu.VMEM(col_desc.shape, col_desc.dtype),
            pltpu.VMEM(col_coords.shape, col_coords.dtype),
            pltpu.SMEM(row_counts.shape, row_counts.dtype),
            pltpu.SMEM(col_counts.shape, col_counts.dtype),
            pltpu.SMEM(row_cluster.shape, row_cluster.dtype),
            pltpu.SMEM(col_cluster.shape, col_cluster.dtype),
            dma((7,)),
            pltpu.VMEM((STEPS // HOP, slots, width), jnp.bfloat16),
            pltpu.VMEM((STEPS // HOP, 2, slots), jnp.bfloat16),
            pltpu.VMEM((STEPS - 1, slots, width), jnp.bfloat16),
            pltpu.VMEM((STEPS - 1, 2, slots), jnp.bfloat16),
            pltpu.VMEM((STEPS, 3, panel, slots), jnp.float32),
            dma((STEPS // HOP, PIECES + 1)),
            dma((STEPS // HOP, PIECES + 1)),
            dma((STEPS - 1, PIECES + 1)),
            dma((STEPS - 1, PIECES + 1)),
            dma((STEPS,)),
            dma((STEPS,)),
        ],
        compiler_params=pltpu.CompilerParams(collective_id=0, has_side_effects=True),
        name="match",
    )(row_counts, col_counts, row_cluster, col_cluster, row_desc, col_desc, col_coords)
    return jnp.transpose(result, (0, 2, 1, 3))


def solution(mesh):
    return jax.shard_map(
        local,
        mesh=mesh,
        in_specs=(
            P(("row", "col"), None, None),
            P(("row", "col"), None, None),
            P(("row", "col"), None, None),
            P(),
            P(),
            P(),
            P(),
        ),
        out_specs=P(None, ("row", "col"), None, None),
        check_vma=False,
    )
```
